32 devices in a mesh: groups: 2 (over x), corpus: 16 (over z, y, core).
Axes of the slice: x: 2, y: 2, z: 4, core: 2. Of those that a mesh axis runs over, the one named last changes fastest.
Arguments:
- queries: bfloat16 [1792, 32, 128], P(('groups', 'corpus')), parts along dimension 0, may hold values from -6 to 6
- passages: bfloat16 [4096, 128, 128], P(('groups', 'corpus')), parts along dimension 0, may hold values from -0.5 to 0.5
- lengths: int32 [4096], P(('groups', 'corpus')), parts along dimension 0, may hold values from 8 to 128
- candidates: int32 [32, 128], P(('groups', 'corpus')), parts along dimension 0, may hold values from 0 to 2047, as said below
Outputs:
- scores: float32 [1792, 128], P(('groups', 'corpus')), parts along dimension 0
- best_scores: float32 [1792, 100], P(('groups', 'corpus')), parts along dimension 0
The draws below stay inside these ranges and needn't reach their ends.
There are 2 independent parts, one for each index of `groups`. The reference program is written for one: setup_inputs(seed, part) draws one part's arguments, and reference() takes and returns one part's arrays. A program takes and returns all parts, laid end to end along the dimension named above; each array names one. Nothing has to cross between parts.
Inputs may be any that keep to these rules, and one draw needn't show every extreme that they name: Row b lists the candidates of queries b * 56 to (b + 1) * 56 - 1. Passage p is held by owner p // 128. In every row at most 12 entries share an owner, and in every row some owner holds exactly 12 of them. Entries may repeat. `lengths`: rows of a tile at or past its length are padding.
All inputs are finite; a program needn't handle non-finite values.
Results may differ from the reference program's by a relative error of at most 0.0003.
Values may be sent and summed in bfloat16 or wider, within the bound.
A program may use at most 128 MiB of HBM per device.

```python
import jax
import jax.numpy as jnp
from jax import lax

D = 128
QTOK = 32
PTOK = 128
CAND = 128
TOPK = 100
Q_DEV = 56
P_DEV = 128
BLOCKS = 16
CAP = 12
QUERIES = 896
PASSAGES = 2048


def draw_candidates(key, part):
    subkeys = jax.random.split(key, 5)
    all_slots = BLOCKS * CAP
    popular = (jax.random.randint(subkeys[0], (BLOCKS,), 0, 8) == 0).astype(jnp.int32)
    leader = jax.random.randint(subkeys[1], (), 0, BLOCKS)
    levels = jnp.where(jnp.arange(BLOCKS) == leader, 2, popular)
    jitter = jax.random.randint(subkeys[2], (BLOCKS, BLOCKS, CAP), 0, 65536)
    slot_score = (jitter + levels[None, :, None] * 65536).reshape(BLOCKS, all_slots)
    slot_score = slot_score * all_slots + jnp.arange(all_slots, dtype=jnp.int32)[None, :]
    picked = lax.top_k(slot_score, CAND)[1]
    owner_of = picked // CAP
    local_id = jax.random.randint(subkeys[3], (BLOCKS, CAND), 0, P_DEV)
    passage_ids = owner_of * P_DEV + local_id
    shuffle_score = jax.random.randint(subkeys[4], (BLOCKS, CAND), 0, 65536) * CAND + jnp.arange(CAND, dtype=jnp.int32)[None, :]
    position = jnp.argsort(shuffle_score, axis=1, stable=True)
    return jnp.take_along_axis(passage_ids, position, axis=1).astype(jnp.int32)


def set_ends(drawn, key, low, top_value):
    index_at = [jax.random.randint(jax.random.fold_in(key, axis), (), 0, length) for axis, length in enumerate(drawn.shape)]
    main_axis = drawn.shape.index(max(drawn.shape))
    neighbour = index_at[:main_axis] + [(index_at[main_axis] + 1) % drawn.shape[main_axis]] + index_at[main_axis + 1:]
    return drawn.at[tuple(index_at)].set(low).at[tuple(neighbour)].set(top_value)


def block_scale(own_key, shape, pieces, least, high):
    loudness = 1.0
    for axis_at, parts in pieces:
        steps = jax.random.uniform(jax.random.fold_in(jax.random.fold_in(own_key, 6), axis_at), (parts,), jnp.float32, least / len(pieces), high / len(pieces))
        loudness = loudness * jnp.repeat(jnp.exp(steps), shape[axis_at] // parts).reshape((-1,) + (1,) * (len(shape) - 1 - axis_at))
    return loudness


def scatter_about(own_key, shape, scale, limit, cuts=(), held_as=jnp.bfloat16):
    result = jax.random.normal(own_key, shape, jnp.float32) * scale
    if len(cuts) > 0:
        result = block_scale(own_key, shape, cuts, -0.22, 0.18) * result
    return jnp.clip(result, min=-limit, max=limit).astype(held_as)


def setup_inputs(seed: int = 0, part: int = 0) -> dict:
    key_list = jax.random.split(jax.random.key(seed), 5)
    part_splits = jax.random.split(jax.random.fold_in(key_list[4], part), 5)
    return {
        "queries": scatter_about(part_splits[0], (QUERIES, QTOK, D), 1.0, 6.0, ((0, 16),)),
        "passages": scatter_about(part_splits[1], (PASSAGES, PTOK, D), D ** -0.5, 0.5, ((0, 16),)),
        "lengths": set_ends(jax.random.randint(part_splits[2], (PASSAGES,), max(1, PTOK // 16), PTOK + 1), jax.random.fold_in(part_splits[2], 1), max(1, PTOK // 16), PTOK).astype(jnp.int32),
        "candidates": draw_candidates(jax.random.fold_in(jax.random.fold_in(key_list[4], part), 71), part),
    }


def reference(queries, passages, lengths, candidates):
    def one_block(block_idx):
        query_rows = lax.dynamic_slice_in_dim(queries, block_idx * Q_DEV, Q_DEV, 0)
        query_rows = query_rows.reshape(Q_DEV * QTOK, D).astype(jnp.float32)
        passage_ids = candidates[block_idx]
        tile_set = passages[passage_ids]
        tile_len = lengths[passage_ids]
        inside = lax.broadcasted_iota(jnp.int32, (CAND, PTOK), 1) < tile_len[:, None]
        tile_set = jnp.where(inside[:, :, None], tile_set, tile_set[:, :1, :]).astype(jnp.float32)
        similar = jnp.einsum('rd,cpd->rcp', query_rows, tile_set)
        nearest = jnp.max(similar, axis=2)
        return jnp.sum(nearest.reshape(Q_DEV, QTOK, CAND), axis=1) / float(QTOK)

    scores = lax.map(one_block, jnp.arange(BLOCKS, dtype=jnp.int32)).reshape(QUERIES, CAND)
    best_scores = lax.top_k(scores, TOPK)[0]
    return scores, best_scores
```

```python
import functools

import jax
import jax.numpy as jnp
from jax import lax
from jax.experimental import pallas as pl
from jax.experimental.pallas import tpu as pltpu
from jax.sharding import PartitionSpec as P

TOPK = 100
MESH = pl.DeviceIdType.MESH


def pick_tile(rows, tok):
    tile = 256
    while rows % tile or tile % tok:
        tile //= 2
    return tile


def kernel(cfg, cand_ref, len_ref, q_hbm, p_hbm, out_ref, qall, pas, cand_all,
           wanted_v, wanted_s, tiles, fold, send_buf, got, q_send, q_recv,
           sib_send, sib_recv, id_send, id_recv, sc_send, sc_recv, loc_sem):
    n, ways, cap, per_owner, tile_rows, rows, feature, tok, col = cfg
    chips = n // 2
    half = chips // 2
    depth = chips // ways
    units = rows // col
    cut = (units + 1) // 2
    spans = ((0, cut), (cut, units))
    me = lax.axis_index("corpus")
    core = lax.rem(me, 2)
    chip = me // 2
    if ways == 2:
        zz, yy = chip // 2, lax.rem(chip, 2)
        pos = (1 - yy) * zz + yy * (2 * depth - 1 - zz)
    else:
        pos = chip

    def at(p, c):
        p = lax.rem(p + 2 * chips, chips)
        if ways == 2:
            far = p // depth
            p = (1 - far) * (2 * p) + far * ((2 * depth - 1 - p) * 2 + 1)
        return p * 2 + c

    sib = at(pos, 1 - core)
    right, left = at(pos + 1, core), at(pos - 1, core)
    toward = (right, left)

    def origin(d, s, c):
        return at(pos - s if d == 0 else pos + s, c)

    def piece(b, k):
        lo, hi = spans[k]
        return qall.at[b, pl.ds(lo * col, (hi - lo) * col), :]

    def hop(d, s, k):
        b = origin(d, s - 1, core)
        return pltpu.make_async_remote_copy(
            src_ref=piece(b, k), dst_ref=piece(b, k),
            send_sem=q_send.at[d, s, k], recv_sem=q_recv.at[d, s, k],
            device_id={"corpus": toward[d]}, device_id_type=MESH)

    def hop_in(d, s, k):
        b = origin(d, s, core)
        return pltpu.make_async_remote_copy(
            src_ref=piece(b, k), dst_ref=piece(b, k),
            send_sem=q_send.at[d, s, k], recv_sem=q_recv.at[d, s, k],
            device_id={"corpus": toward[d]}, device_id_type=MESH)

    def share(d, s, k, c):
        b = origin(d, s, c)
        return pltpu.make_async_remote_copy(
            src_ref=piece(b, k), dst_ref=piece(b, k),
            send_sem=sib_send.at[d, s, k], recv_sem=sib_recv.at[d, s, k],
            device_id={"corpus": sib}, device_id_type=MESH)

    def has_hop(d, s, k):
        return 1 <= s < half or (s == half and k == d)

    def id_copy(o):
        peer = lax.rem(me + o, n)
        return pltpu.make_async_remote_copy(
            src_ref=cand_all.at[me], dst_ref=cand_all.at[me],
            send_sem=id_send.at[o], recv_sem=id_recv.at[me],
            device_id={"corpus": peer}, device_id_type=MESH)

    def id_in(o):
        peer = lax.rem(me + o, n)
        return pltpu.make_async_remote_copy(
            src_ref=cand_all.at[peer], dst_ref=cand_all.at[peer],
            send_sem=id_send.at[o], recv_sem=id_recv.at[peer],
            device_id={"corpus": peer}, device_id_type=MESH)

    def score_copy(b):
        return pltpu.make_async_remote_copy(
            src_ref=send_buf.at[b], dst_ref=got.at[me],
            send_sem=sc_send.at[b], recv_sem=sc_recv.at[me],
            device_id={"corpus": b}, device_id_type=MESH)

    def score_in(o):
        peer = lax.rem(me + o, n)
        return pltpu.make_async_remote_copy(
            src_ref=send_buf.at[peer], dst_ref=got.at[peer],
            send_sem=sc_send.at[peer], recv_sem=sc_recv.at[peer],
            device_id={"corpus": peer}, device_id_type=MESH)

    q_load = pltpu.make_async_copy(q_hbm, qall.at[me], loc_sem.at[0])
    c_load = pltpu.make_async_copy(cand_ref, cand_all.at[me], loc_sem.at[2])
    p_load = pltpu.make_async_copy(p_hbm, pas, loc_sem.at[1])
    c_load.start()
    q_load.start()
    p_load.start()

    barrier = pltpu.get_barrier_semaphore()

    def greet(o, _):
        pl.semaphore_signal(barrier, inc=1, device_id={"corpus": lax.rem(me + o, n)},
                            device_id_type=MESH)
        return 0

    lax.fori_loop(1, n, greet, 0)
    row_at = lax.broadcasted_iota(jnp.int32, (rows, 128), 0) // tok
    lane_at = lax.broadcasted_iota(jnp.int32, (rows, 128), 1)
    fold[...] = jnp.where(row_at == lane_at, 1.0, 0.0).astype(fold.dtype)
    c_load.wait()
    q_load.wait()
    pl.semaphore_wait(barrier, n - 1)

    def each(first, fn):
        def body(o, _):
            fn(o)
            return 0
        lax.fori_loop(first, n, body, 0)

    each(1, lambda o: id_copy(o).start())
    for k in range(2):
        for d in range(2):
            if has_hop(d, 1, k):
                hop(d, 1, k).start()
        share(0, 0, k, core).start()
    each(1, lambda o: id_in(o).wait_recv())

    ids = cand_all[...].reshape(n, cand_all.shape[2])
    number = ids.shape[1]
    owner = lax.div(ids, per_owner)
    local = ids - owner * per_owner
    mine = owner == me
    r_at = lax.broadcasted_iota(jnp.int32, (number, number), 0)
    c_at = lax.broadcasted_iota(jnp.int32, (number, number), 1)
    before = jnp.where(r_at < c_at, 1.0, 0.0).astype(jnp.bfloat16)
    rank = jnp.dot(jnp.where(mine, 1.0, 0.0).astype(jnp.bfloat16), before,
                   preferred_element_type=jnp.float32)
    lane = lax.broadcasted_iota(jnp.int32, (n, number), 1)
    wanted = jnp.zeros((n, number), jnp.int32)
    for s in range(cap):
        hit = mine & (rank == float(s))
        found = jnp.max(jnp.where(hit, local, 0), axis=1, keepdims=True)
        wanted = jnp.where(lane == s, found, wanted)
    wanted_v[...] = wanted
    w_load = pltpu.make_async_copy(wanted_v, wanted_s, loc_sem.at[3])
    w_load.start()
    p_load.wait()
    w_load.wait()

    in_tile = lax.broadcasted_iota(jnp.int32, (tile_rows, feature), 0)
    slots = send_buf.shape[1]

    def compute(b, k):
        for s in range(cap):
            chosen = wanted_s[b, s]
            tile = pas[chosen].astype(jnp.float32)
            tile = jnp.where(in_tile < len_ref[chosen], tile, tile[0:1, :])
            tiles[pl.ds(s * tile_rows, tile_rows), :] = tile.astype(tiles.dtype)
        total = None
        for u in range(*spans[k]):
            qs = qall[b, pl.ds(u * col, col), :]
            near = []
            for s in range(cap):
                sim = lax.dot_general(
                    tiles[pl.ds(s * tile_rows, tile_rows), :], qs,
                    (((1,), (1,)), ((), ())), preferred_element_type=jnp.float32)
                near.append(jnp.max(sim, axis=0, keepdims=True))
            if cap < slots:
                near.append(jnp.zeros((slots - cap, col), jnp.float32))
            near = jnp.concatenate(near, axis=0)
            high = near.astype(jnp.bfloat16).astype(jnp.float32)
            both = jnp.concatenate([high, near - high], axis=0).astype(jnp.bfloat16)
            part = jnp.dot(both, fold[pl.ds(u * col, col), :],
                           preferred_element_type=jnp.float32)
            part = part[:slots] + part[slots:]
            total = part if total is None else total + part
        total = total / float(tok)
        if k == 0:
            send_buf[b] = total
        else:
            send_buf[b] = send_buf[b] + total

    for k in range(2):
        share(0, 0, k, 1 - core).wait_recv()

    def near_body(j, _):
        b = at(pos, lax.rem(core + j, 2))
        for k in range(2):
            compute(b, k)

        @pl.when(j == 1)
        def _():
            score_copy(b).start()
        return 0

    lax.fori_loop(0, 2, near_body, 0)
    got[me] = send_buf[me]

    for s in range(1, half):
        for k in range(2):
            for d in range(2):
                hop_in(d, s, k).wait_recv()
                if has_hop(d, s + 1, k):
                    hop(d, s + 1, k).start()
                share(d, s, k, core).start()

            def ring_body(j, _, s=s, k=k):
                far = j // 2
                away = lax.rem(j, 2)
                step = (2 * away - 1) * s
                b = at(pos + step, lax.rem(core + far, 2))

                @pl.when(j == 2)
                def _():
                    for d in range(2):
                        share(d, s, k, 1 - core).wait_recv()
                compute(b, k)
                if k == 1:
                    score_copy(b).start()
                return 0

            lax.fori_loop(0, 4, ring_body, 0)
    for k in range(2):
        hop_in(k, half, k).wait_recv()
        share(k, half, k, core).start()

    def last_body(j, _):
        b = at(pos + half, lax.rem(core + j, 2))

        @pl.when(j == 1)
        def _():
            for k in range(2):
                share(k, half, k, 1 - core).wait_recv()
        for k in range(2):
            compute(b, k)
        score_copy(b).start()
        return 0

    lax.fori_loop(0, 2, last_body, 0)

    for k in range(2):
        share(0, 0, k, core).wait_send()
        for d in range(2):
            for s in range(1, half + 1):
                if has_hop(d, s, k):
                    hop(d, s, k).wait_send()
                    share(d, s, k, core).wait_send()
    each(1, lambda o: id_copy(o).wait_send())
    each(1, lambda o: score_copy(lax.rem(me + o, n)).wait_send())
    each(1, lambda o: score_in(o).wait_recv())
    out_ref[...] = got[...]


def local(ways, queries, passages, lengths, candidates):
    n = lax.axis_size("corpus")
    per_owner, tile_rows, feature = passages.shape
    per_device, tok = queries.shape[0], queries.shape[1]
    number = candidates.shape[1]
    rows = per_device * tok
    cap = max(2, 3 * number // (2 * n))
    slots = -(-cap // 8) * 8
    col = pick_tile(rows, tok)
    half = n // 4
    cfg = (n, ways, cap, per_owner, tile_rows, rows, feature, tok, col)
    got = pl.pallas_call(
        functools.partial(kernel, cfg),
        out_shape=jax.ShapeDtypeStruct((n, slots, 128), jnp.float32),
        in_specs=[
            pl.BlockSpec(memory_space=pltpu.VMEM),
            pl.BlockSpec(memory_space=pltpu.SMEM),
            pl.BlockSpec(memory_space=pl.ANY),
            pl.BlockSpec(memory_space=pl.ANY),
        ],
        out_specs=pl.BlockSpec(memory_space=pltpu.VMEM),
        scratch_shapes=[
            pltpu.VMEM((n, rows, feature), queries.dtype),
            pltpu.VMEM(passages.shape, passages.dtype),
            pltpu.VMEM((n, 1, number), jnp.int32),
            pltpu.VMEM((n, number), jnp.int32),
            pltpu.SMEM((n, number), jnp.int32),
            pltpu.VMEM((cap * tile_rows, feature), passages.dtype),
            pltpu.VMEM((rows, 128), jnp.bfloat16),
            pltpu.VMEM((n, slots, 128), jnp.float32),
            pltpu.VMEM((n, slots, 128), jnp.float32),
            pltpu.SemaphoreType.DMA((2, half + 1, 2)),
            pltpu.SemaphoreType.DMA((2, half + 1, 2)),
            pltpu.SemaphoreType.DMA((2, half + 1, 2)),
            pltpu.SemaphoreType.DMA((2, half + 1, 2)),
            pltpu.SemaphoreType.DMA((n,)),
            pltpu.SemaphoreType.DMA((n,)),
            pltpu.SemaphoreType.DMA((n,)),
            pltpu.SemaphoreType.DMA((n,)),
            pltpu.SemaphoreType.DMA((4,)),
        ],
        compiler_params=pltpu.CompilerParams(
            collective_id=0, has_side_effects=True, vmem_limit_bytes=60 * 2**20),
    )(candidates, lengths, queries.reshape(rows, feature), passages)

    ids = candidates[0]
    owner_of = ids // per_owner
    position = jnp.arange(number, dtype=jnp.int32)
    shared = (owner_of[:, None] == owner_of[None, :]) & (position[None, :] < position[:, None])
    slot_of = owner_of * slots + jnp.sum(shared.astype(jnp.int32), axis=1)
    picked = jnp.take(got.reshape(n * slots, 128), slot_of, axis=0)
    scores = picked.T[:per_device]
    best_scores = lax.top_k(scores, TOPK)[0]
    return (scores, best_scores)


def solution(mesh):
    ways = 2 if mesh.shape["groups"] == 2 else 1
    return jax.shard_map(
        functools.partial(local, ways),
        mesh=mesh,
        in_specs=(
            P(("groups", "corpus"), None, None),
            P(("groups", "corpus"), None, None),
            P(("groups", "corpus")),
            P(("groups", "corpus"), None),
        ),
        out_specs=(P(("groups", "corpus"), None), P(("groups", "corpus"), None)),
        check_vma=False,
    )
```

```python
import functools

import jax
import jax.numpy as jnp
from jax import lax
from jax.experimental import pallas as pl
from jax.experimental.pallas import tpu as pltpu
from jax.sharding import PartitionSpec as P

TOPK = 100
MESH = pl.DeviceIdType.MESH


def pick_tile(rows, tok):
    tile = 256
    while rows % tile or tile % tok:
        tile //= 2
    return tile


def sort_down(x):
    count, width = x.shape
    index = lax.broadcasted_iota(jnp.int32, (count // 8, 8, width), 0) * 8
    index = index + lax.broadcasted_iota(jnp.int32, (count // 8, 8, width), 1)
    x = x.reshape(count // 8, 8, width)
    size = 2
    while size <= count:
        gap = size // 2
        falling = (index // size) % 2 == 0
        while gap >= 1:
            low = (index // gap) % 2 == 0
            if gap >= 8:
                hop = gap // 8
                y = x.reshape(count // (2 * gap), 2, hop, 8, width)
                y = jnp.concatenate([y[:, 1:], y[:, :1]], axis=1)
                other = y.reshape(x.shape)
            else:
                other = jnp.where(low, pltpu.roll(x, 8 - gap, 1), pltpu.roll(x, gap, 1))
            x = jnp.where(low == falling, jnp.maximum(x, other), jnp.minimum(x, other))
            gap //= 2
        size *= 2
    return x.reshape(count, width)


def split3(x):
    high = x.astype(jnp.bfloat16)
    rest = x - high.astype(jnp.float32)
    mid = rest.astype(jnp.bfloat16)
    low = (rest - mid.astype(jnp.float32)).astype(jnp.bfloat16)
    return high, mid, low


def kernel(cfg, cand_ref, len_ref, q_hbm, p_hbm, out_ref, best_ref, qall, pas, cand_all,
           wanted_v, wanted_s, place, fold, send_buf, got, q_send, q_recv,
           sib_send, sib_recv, id_send, id_recv, sc_send, sc_recv, loc_sem):
    n, ways, cap, per_owner, tile_rows, rows, feature, tok, col = cfg
    chips = n // 2
    half = chips // 2
    depth = chips // ways
    units = rows // col
    cut = (units + 1) // 2
    spans = ((0, cut), (cut, units))
    me = lax.axis_index("corpus")
    core = lax.rem(me, 2)
    chip = me // 2
    if ways == 2:
        zz, yy = chip // 2, lax.rem(chip, 2)
        pos = (1 - yy) * zz + yy * (2 * depth - 1 - zz)
    else:
        pos = chip

    def at(p, c):
        p = lax.rem(p + 2 * chips, chips)
        if ways == 2:
            far = p // depth
            p = (1 - far) * (2 * p) + far * ((2 * depth - 1 - p) * 2 + 1)
        return p * 2 + c

    sib = at(pos, 1 - core)
    right, left = at(pos + 1, core), at(pos - 1, core)
    toward = (right, left)

    def origin(d, s, c):
        return at(pos - s if d == 0 else pos + s, c)

    def piece(b, k):
        lo, hi = spans[k]
        return qall.at[b, pl.ds(lo * col, (hi - lo) * col), :]

    def hop(d, s, k):
        b = origin(d, s - 1, core)
        return pltpu.make_async_remote_copy(
            src_ref=piece(b, k), dst_ref=piece(b, k),
            send_sem=q_send.at[d, s, k], recv_sem=q_recv.at[d, s, k],
            device_id={"corpus": toward[d]}, device_id_type=MESH)

    def hop_in(d, s, k):
        b = origin(d, s, core)
        return pltpu.make_async_remote_copy(
            src_ref=piece(b, k), dst_ref=piece(b, k),
            send_sem=q_send.at[d, s, k], recv_sem=q_recv.at[d, s, k],
            device_id={"corpus": toward[d]}, device_id_type=MESH)

    def share(d, s, k, c):
        b = origin(d, s, c)
        return pltpu.make_async_remote_copy(
            src_ref=piece(b, k), dst_ref=piece(b, k),
            send_sem=sib_send.at[d, s, k], recv_sem=sib_recv.at[d, s, k],
            device_id={"corpus": sib}, device_id_type=MESH)

    def has_hop(d, s, k):
        return 1 <= s < half or (s == half and k == d)

    def id_copy(o):
        peer = lax.rem(me + o, n)
        return pltpu.make_async_remote_copy(
            src_ref=cand_all.at[me], dst_ref=cand_all.at[me],
            send_sem=id_send.at[o], recv_sem=id_recv.at[me],
            device_id={"corpus": peer}, device_id_type=MESH)

    def id_in(o):
        peer = lax.rem(me + o, n)
        return pltpu.make_async_remote_copy(
            src_ref=cand_all.at[peer], dst_ref=cand_all.at[peer],
            send_sem=id_send.at[o], recv_sem=id_recv.at[peer],
            device_id={"corpus": peer}, device_id_type=MESH)

    def score_copy(b):
        return pltpu.make_async_remote_copy(
            src_ref=send_buf.at[b], dst_ref=got.at[me],
            send_sem=sc_send.at[b], recv_sem=sc_recv.at[me],
            device_id={"corpus": b}, device_id_type=MESH)

    def score_in(o):
        peer = lax.rem(me + o, n)
        return pltpu.make_async_remote_copy(
            src_ref=send_buf.at[peer], dst_ref=got.at[peer],
            send_sem=sc_send.at[peer], recv_sem=sc_recv.at[peer],
            device_id={"corpus": peer}, device_id_type=MESH)

    q_load = pltpu.make_async_copy(q_hbm, qall.at[me], loc_sem.at[0])
    c_load = pltpu.make_async_copy(cand_ref, cand_all.at[me], loc_sem.at[2])
    p_load = pltpu.make_async_copy(p_hbm, pas, loc_sem.at[1])
    c_load.start()
    q_load.start()
    p_load.start()

    barrier = pltpu.get_barrier_semaphore()

    def greet(o, _):
        pl.semaphore_signal(barrier, inc=1, device_id={"corpus": lax.rem(me + o, n)},
                            device_id_type=MESH)
        return 0

    lax.fori_loop(1, n, greet, 0)
    row_at = lax.broadcasted_iota(jnp.int32, (rows, 128), 0) // tok
    lane_at = lax.broadcasted_iota(jnp.int32, (rows, 128), 1)
    fold[...] = jnp.where(row_at == lane_at, 1.0, 0.0).astype(fold.dtype)
    slots = send_buf.shape[1]
    number = cand_ref.shape[1]
    mine_row = lax.div(cand_ref[...], per_owner).astype(jnp.float32)
    across = jnp.broadcast_to(mine_row, (number, number))
    down = across.T
    r_at = lax.broadcasted_iota(jnp.int32, (number, number), 0)
    c_at = lax.broadcasted_iota(jnp.int32, (number, number), 1)
    ahead = jnp.where((across == down) & (c_at < r_at), 1.0, 0.0)
    slot = down[:, :1] * float(slots) + jnp.sum(ahead, axis=1, keepdims=True)
    slot_at = lax.broadcasted_iota(jnp.int32, place.shape, 1).astype(jnp.float32)
    place[...] = jnp.where(slot_at == slot, 1.0, 0.0).astype(place.dtype)
    c_load.wait()
    q_load.wait()
    pl.semaphore_wait(barrier, n - 1)

    def each(first, fn):
        def body(o, _):
            fn(o)
            return 0
        lax.fori_loop(first, n, body, 0)

    each(1, lambda o: id_copy(o).start())
    for k in range(2):
        for d in range(2):
            if has_hop(d, 1, k):
                hop(d, 1, k).start()
        share(0, 0, k, core).start()
    in_tile = lax.broadcasted_iota(jnp.int32, (tile_rows, feature), 0)
    p_load.wait()

    def fill(i, _):
        for j in range(4):
            p = i * 4 + j
            tile = pas[p].astype(jnp.float32)
            tile = jnp.where(in_tile < len_ref[p], tile, tile[0:1, :])
            pas[p] = tile.astype(pas.dtype)
        return 0

    lax.fori_loop(0, per_owner // 4, fill, 0)
    each(1, lambda o: id_in(o).wait_recv())

    ids = cand_all[...].reshape(n, cand_all.shape[2])
    owner = lax.div(ids, per_owner)
    local = ids - owner * per_owner
    mine = owner == me
    before = jnp.where(r_at < c_at, 1.0, 0.0).astype(jnp.bfloat16)
    rank = jnp.dot(jnp.where(mine, 1.0, 0.0).astype(jnp.bfloat16), before,
                   preferred_element_type=jnp.float32)
    lane = lax.broadcasted_iota(jnp.int32, (n, number), 1)
    wanted = jnp.zeros((n, number), jnp.int32)
    for s in range(cap):
        hit = mine & (rank == float(s))
        found = jnp.max(jnp.where(hit, local, 0), axis=1, keepdims=True)
        wanted = jnp.where(lane == s, found, wanted)
    wanted_v[...] = wanted
    w_load = pltpu.make_async_copy(wanted_v, wanted_s, loc_sem.at[3])
    w_load.start()
    w_load.wait()

    def compute(b, k):
        chosen = [wanted_s[b, s] for s in range(cap)]
        pieces = []
        for u in range(*spans[k]):
            qs = qall[b, pl.ds(u * col, col), :]
            near = []
            for s in range(cap):
                sim = lax.dot_general(pas[chosen[s]], qs, (((1,), (1,)), ((), ())),
                                      preferred_element_type=jnp.float32)
                near.append(jnp.max(sim, axis=0, keepdims=True))
            if cap < slots:
                near.append(jnp.zeros((slots - cap, col), jnp.float32))
            near = jnp.concatenate(near, axis=0)
            high = near.astype(jnp.bfloat16).astype(jnp.float32)
            pieces.append(jnp.concatenate([high, near - high], axis=0).astype(jnp.bfloat16))
        lo, hi = spans[k]
        part = jnp.dot(jnp.concatenate(pieces, axis=1), fold[pl.ds(lo * col, (hi - lo) * col), :],
                       preferred_element_type=jnp.float32)
        return (part[:slots] + part[slots:]) / float(tok)

    for k in range(2):
        share(0, 0, k, 1 - core).wait_recv()

    def near_body(j, _):
        b = at(pos, lax.rem(core + j, 2))
        send_buf[b] = compute(b, 0) + compute(b, 1)

        @pl.when(j == 1)
        def _():
            score_copy(b).start()
        return 0

    lax.fori_loop(0, 2, near_body, 0)
    got[me] = send_buf[me]

    for s in range(1, half):
        for k in range(2):
            for d in range(2):
                hop_in(d, s, k).wait_recv()
                if has_hop(d, s + 1, k):
                    hop(d, s + 1, k).start()
                share(d, s, k, core).start()

            def ring_body(j, _, s=s, k=k):
                @pl.when(j == 1)
                def _():
                    for d in range(2):
                        share(d, s, k, 1 - core).wait_recv()
                blocks = [origin(d, s, lax.rem(core + j, 2)) for d in range(2)]
                found = [compute(b, k) for b in blocks]
                for b, part in zip(blocks, found):
                    send_buf[b] = part if k == 0 else send_buf[b] + part
                if k == 1:
                    for b in blocks:
                        score_copy(b).start()
                return 0

            lax.fori_loop(0, 2, ring_body, 0)
    for k in range(2):
        hop_in(k, half, k).wait_recv()
        share(k, half, k, core).start()

    def last_body(j, _):
        b = at(pos + half, lax.rem(core + j, 2))

        @pl.when(j == 1)
        def _():
            for k in range(2):
                share(k, half, k, 1 - core).wait_recv()
        send_buf[b] = compute(b, 0) + compute(b, 1)
        score_copy(b).start()
        return 0

    lax.fori_loop(0, 2, last_body, 0)

    for k in range(2):
        share(0, 0, k, core).wait_send()
        for d in range(2):
            for s in range(1, half + 1):
                if has_hop(d, s, k):
                    hop(d, s, k).wait_send()
                    share(d, s, k, core).wait_send()
    each(1, lambda o: id_copy(o).wait_send())
    each(1, lambda o: score_copy(lax.rem(me + o, n)).wait_send())
    each(1, lambda o: score_in(o).wait_recv())
    flat = got[...].reshape(n * slots, got.shape[2])
    spread = None
    for part in split3(flat):
        term = jnp.dot(place[...], part, preferred_element_type=jnp.float32)
        spread = term if spread is None else spread + term
    queries = out_ref.shape[0]
    out_ref[...] = spread.T[:queries]
    best_ref[...] = sort_down(spread).T[:queries, :best_ref.shape[1]]


def local(ways, queries, passages, lengths, candidates):
    n = lax.axis_size("corpus")
    per_owner, tile_rows, feature = passages.shape
    per_device, tok = queries.shape[0], queries.shape[1]
    number = candidates.shape[1]
    rows = per_device * tok
    cap = max(2, 3 * number // (2 * n))
    slots = -(-cap // 8) * 8
    col = pick_tile(rows, tok)
    half = n // 4
    cfg = (n, ways, cap, per_owner, tile_rows, rows, feature, tok, col)
    return pl.pallas_call(
        functools.partial(kernel, cfg),
        out_shape=(
            jax.ShapeDtypeStruct((per_device, number), jnp.float32),
            jax.ShapeDtypeStruct((per_device, TOPK), jnp.float32),
        ),
        in_specs=[
            pl.BlockSpec(memory_space=pltpu.VMEM),
            pl.BlockSpec(memory_space=pltpu.SMEM),
            pl.BlockSpec(memory_space=pl.ANY),
            pl.BlockSpec(memory_space=pl.ANY),
        ],
        out_specs=(
            pl.BlockSpec(memory_space=pltpu.VMEM),
            pl.BlockSpec(memory_space=pltpu.VMEM),
        ),
        scratch_shapes=[
            pltpu.VMEM((n, rows, feature), queries.dtype),
            pltpu.VMEM(passages.shape, passages.dtype),
            pltpu.VMEM((n, 1, number), jnp.int32),
            pltpu.VMEM((n, number), jnp.int32),
            pltpu.SMEM((n, number), jnp.int32),
            pltpu.VMEM((number, n * slots), jnp.bfloat16),
            pltpu.VMEM((rows, 128), jnp.bfloat16),
            pltpu.VMEM((n, slots, 128), jnp.float32),
            pltpu.VMEM((n, slots, 128), jnp.float32),
            pltpu.SemaphoreType.DMA((2, half + 1, 2)),
            pltpu.SemaphoreType.DMA((2, half + 1, 2)),
            pltpu.SemaphoreType.DMA((2, half + 1, 2)),
            pltpu.SemaphoreType.DMA((2, half + 1, 2)),
            pltpu.SemaphoreType.DMA((n,)),
            pltpu.SemaphoreType.DMA((n,)),
            pltpu.SemaphoreType.DMA((n,)),
            pltpu.SemaphoreType.DMA((n,)),
            pltpu.SemaphoreType.DMA((4,)),
        ],
        compiler_params=pltpu.CompilerParams(
            collective_id=0, has_side_effects=True, vmem_limit_bytes=60 * 2**20),
    )(candidates, lengths, queries.reshape(rows, feature), passages)


def solution(mesh):
    ways = 2 if mesh.shape["groups"] == 2 else 1
    return jax.shard_map(
        functools.partial(local, ways),
        mesh=mesh,
        in_specs=(
            P(("groups", "corpus"), None, None),
            P(("groups", "corpus"), None, None),
            P(("groups", "corpus")),
            P(("groups", "corpus"), None),
        ),
        out_specs=(P(("groups", "corpus"), None), P(("groups", "corpus"), None)),
        check_vma=False,
    )
```

```python
import functools

import jax
import jax.numpy as jnp
from jax import lax
from jax.experimental import pallas as pl
from jax.experimental.pallas import tpu as pltpu
from jax.sharding import PartitionSpec as P

TOPK = 100
MESH = pl.DeviceIdType.MESH


def pick_tile(rows, tok):
    tile = 256
    while rows % tile or tile % tok:
        tile //= 2
    return tile


def sort_down(x):
    count, width = x.shape
    index = lax.broadcasted_iota(jnp.int32, (count // 8, 8, width), 0) * 8
    index = index + lax.broadcasted_iota(jnp.int32, (count // 8, 8, width), 1)
    x = x.reshape(count // 8, 8, width)
    size = 2
    while size <= count:
        gap = size // 2
        falling = (index // size) % 2 == 0
        while gap >= 1:
            low = (index // gap) % 2 == 0
            if gap >= 8:
                hop = gap // 8
                y = x.reshape(count // (2 * gap), 2, hop, 8, width)
                y = jnp.concatenate([y[:, 1:], y[:, :1]], axis=1)
                other = y.reshape(x.shape)
            else:
                other = jnp.where(low, pltpu.roll(x, 8 - gap, 1), pltpu.roll(x, gap, 1))
            x = jnp.where(low == falling, jnp.maximum(x, other), jnp.minimum(x, other))
            gap //= 2
        size *= 2
    return x.reshape(count, width)


def split3(x):
    high = x.astype(jnp.bfloat16)
    rest = x - high.astype(jnp.float32)
    mid = rest.astype(jnp.bfloat16)
    low = (rest - mid.astype(jnp.float32)).astype(jnp.bfloat16)
    return high, mid, low


def kernel(cfg, cand_ref, len_ref, q_hbm, p_hbm, out_ref, place_ref, qall, pas, cand_all,
           wanted_v, wanted_s, place, fold, send_buf, got, q_send, q_recv,
           sib_send, sib_recv, id_send, id_recv, sc_send, sc_recv, loc_sem):
    n, ways, cap, per_owner, tile_rows, rows, feature, tok, col = cfg
    chips = n // 2
    half = chips // 2
    depth = chips // ways
    units = rows // col
    cut = (units + 1) // 2
    spans = ((0, cut), (cut, units))
    ends = tuple(((lo, (lo + hi + 1) // 2), ((lo + hi + 1) // 2, hi)) for lo, hi in spans)
    me = lax.axis_index("corpus")
    core = lax.rem(me, 2)
    chip = me // 2
    if ways == 2:
        zz, yy = chip // 2, lax.rem(chip, 2)
        pos = (1 - yy) * zz + yy * (2 * depth - 1 - zz)
    else:
        pos = chip

    def at(p, c):
        p = lax.rem(p + 2 * chips, chips)
        if ways == 2:
            far = p // depth
            p = (1 - far) * (2 * p) + far * ((2 * depth - 1 - p) * 2 + 1)
        return p * 2 + c

    sib = at(pos, 1 - core)
    right, left = at(pos + 1, core), at(pos - 1, core)
    toward = (right, left)

    def origin(d, s, c):
        return at(pos - s if d == 0 else pos + s, c)

    def piece(b, d, s, k):
        lo, hi = ends[d][k] if s == half else spans[k]
        return qall.at[b, pl.ds(lo * col, (hi - lo) * col), :]

    def hop(d, s, k):
        b = origin(d, s - 1, core)
        return pltpu.make_async_remote_copy(
            src_ref=piece(b, d, s, k), dst_ref=piece(b, d, s, k),
            send_sem=q_send.at[d, s, k], recv_sem=q_recv.at[d, s, k],
            device_id={"corpus": toward[d]}, device_id_type=MESH)

    def hop_in(d, s, k):
        b = origin(d, s, core)
        return pltpu.make_async_remote_copy(
            src_ref=piece(b, d, s, k), dst_ref=piece(b, d, s, k),
            send_sem=q_send.at[d, s, k], recv_sem=q_recv.at[d, s, k],
            device_id={"corpus": toward[d]}, device_id_type=MESH)

    def share(d, s, k, c):
        b = origin(d, s, c)
        return pltpu.make_async_remote_copy(
            src_ref=piece(b, d, s, k), dst_ref=piece(b, d, s, k),
            send_sem=sib_send.at[d, s, k], recv_sem=sib_recv.at[d, s, k],
            device_id={"corpus": sib}, device_id_type=MESH)

    def id_copy(o):
        peer = lax.rem(me + o, n)
        return pltpu.make_async_remote_copy(
            src_ref=cand_all.at[me], dst_ref=cand_all.at[me],
            send_sem=id_send.at[o], recv_sem=id_recv.at[me],
            device_id={"corpus": peer}, device_id_type=MESH)

    def id_in(o):
        peer = lax.rem(me + o, n)
        return pltpu.make_async_remote_copy(
            src_ref=cand_all.at[peer], dst_ref=cand_all.at[peer],
            send_sem=id_send.at[o], recv_sem=id_recv.at[peer],
            device_id={"corpus": peer}, device_id_type=MESH)

    def score_copy(b):
        return pltpu.make_async_remote_copy(
            src_ref=send_buf.at[b], dst_ref=got.at[me],
            send_sem=sc_send.at[b], recv_sem=sc_recv.at[me],
            device_id={"corpus": b}, device_id_type=MESH)

    def score_in(o):
        peer = lax.rem(me + o, n)
        return pltpu.make_async_remote_copy(
            src_ref=send_buf.at[peer], dst_ref=got.at[peer],
            send_sem=sc_send.at[peer], recv_sem=sc_recv.at[peer],
            device_id={"corpus": peer}, device_id_type=MESH)

    q_load = pltpu.make_async_copy(q_hbm, qall.at[me], loc_sem.at[0])
    c_load = pltpu.make_async_copy(cand_ref, cand_all.at[me], loc_sem.at[2])
    p_load = pltpu.make_async_copy(p_hbm, pas, loc_sem.at[1])
    c_load.start()
    q_load.start()
    p_load.start()

    barrier = pltpu.get_barrier_semaphore()

    def greet(o, _):
        pl.semaphore_signal(barrier, inc=1, device_id={"corpus": lax.rem(me + o, n)},
                            device_id_type=MESH)
        return 0

    lax.fori_loop(1, n, greet, 0)
    row_at = lax.broadcasted_iota(jnp.int32, (rows, 128), 0) // tok
    lane_at = lax.broadcasted_iota(jnp.int32, (rows, 128), 1)
    fold[...] = jnp.where(row_at == lane_at, 1.0, 0.0).astype(fold.dtype)
    slots = send_buf.shape[1]
    number = cand_ref.shape[1]
    mine_row = lax.div(cand_ref[...], per_owner).astype(jnp.float32)
    across = jnp.broadcast_to(mine_row, (number, number))
    down = across.T
    r_at = lax.broadcasted_iota(jnp.int32, (number, number), 0)
    c_at = lax.broadcasted_iota(jnp.int32, (number, number), 1)
    ahead = jnp.where((across == down) & (c_at < r_at), 1.0, 0.0)
    slot = down[:, :1] * float(slots) + jnp.sum(ahead, axis=1, keepdims=True)
    slot_at = lax.broadcasted_iota(jnp.int32, place.shape, 1).astype(jnp.float32)
    place[...] = jnp.where(slot_at == slot, 1.0, 0.0).astype(place.dtype)
    c_load.wait()
    q_load.wait()
    pl.semaphore_wait(barrier, n - 1)

    def each(first, fn):
        def body(o, _):
            fn(o)
            return 0
        lax.fori_loop(first, n, body, 0)

    each(1, lambda o: id_copy(o).start())
    for k in range(2):
        for d in range(2):
            hop(d, 1, k).start()
        share(0, 0, k, core).start()
    in_tile = lax.broadcasted_iota(jnp.int32, (tile_rows, feature), 0)
    p_load.wait()

    def fill(i, _):
        for j in range(4):
            p = i * 4 + j
            tile = pas[p].astype(jnp.float32)
            tile = jnp.where(in_tile < len_ref[p], tile, tile[0:1, :])
            pas[p] = tile.astype(pas.dtype)
        return 0

    lax.fori_loop(0, per_owner // 4, fill, 0)
    each(1, lambda o: id_in(o).wait_recv())

    ids = cand_all[...].reshape(n, cand_all.shape[2])
    owner = lax.div(ids, per_owner)
    local = ids - owner * per_owner
    mine = owner == me
    before = jnp.where(r_at < c_at, 1.0, 0.0).astype(jnp.bfloat16)
    rank = jnp.dot(jnp.where(mine, 1.0, 0.0).astype(jnp.bfloat16), before,
                   preferred_element_type=jnp.float32)
    lane = lax.broadcasted_iota(jnp.int32, (n, number), 1)
    wanted = jnp.zeros((n, number), jnp.int32)
    for s in range(cap):
        hit = mine & (rank == float(s))
        found = jnp.max(jnp.where(hit, local, 0), axis=1, keepdims=True)
        wanted = jnp.where(lane == s, found, wanted)
    wanted_v[...] = wanted
    w_load = pltpu.make_async_copy(wanted_v, wanted_s, loc_sem.at[3])
    w_load.start()
    w_load.wait()

    def compute(b, lo, hi):
        chosen = [wanted_s[b, s] for s in range(cap)]
        pieces = []
        for u in range(lo, hi):
            qs = qall[b, pl.ds(u * col, col), :]
            near = []
            for s in range(cap):
                sim = lax.dot_general(pas[chosen[s]], qs, (((1,), (1,)), ((), ())),
                                      preferred_element_type=jnp.float32)
                near.append(jnp.max(sim, axis=0, keepdims=True))
            if cap < slots:
                near.append(jnp.zeros((slots - cap, col), jnp.float32))
            near = jnp.concatenate(near, axis=0)
            high = near.astype(jnp.bfloat16).astype(jnp.float32)
            pieces.append(jnp.concatenate([high, near - high], axis=0).astype(jnp.bfloat16))
        part = jnp.dot(jnp.concatenate(pieces, axis=1), fold[pl.ds(lo * col, (hi - lo) * col), :],
                       preferred_element_type=jnp.float32)
        return (part[:slots] + part[slots:]) / float(tok)

    for k in range(2):
        share(0, 0, k, 1 - core).wait_recv()

    def near_body(j, _):
        b = at(pos, lax.rem(core + j, 2))
        send_buf[b] = compute(b, *spans[0]) + compute(b, *spans[1])

        @pl.when(j == 1)
        def _():
            score_copy(b).start()
        return 0

    lax.fori_loop(0, 2, near_body, 0)
    got[me] = send_buf[me]

    for s in range(1, half):
        for k in range(2):
            for d in range(2):
                hop_in(d, s, k).wait_recv()
                if s + 1 < half:
                    hop(d, s + 1, k).start()
                elif k == d:
                    for m in range(2):
                        hop(d, half, m).start()
                share(d, s, k, core).start()

            def ring_body(j, _, s=s, k=k):
                @pl.when(j == 1)
                def _():
                    for d in range(2):
                        share(d, s, k, 1 - core).wait_recv()
                blocks = [origin(d, s, lax.rem(core + j, 2)) for d in range(2)]
                found = [compute(b, *spans[k]) for b in blocks]
                for b, part in zip(blocks, found):
                    send_buf[b] = part if k == 0 else send_buf[b] + part
                if k == 1:
                    for b in blocks:
                        score_copy(b).start()
                return 0

            lax.fori_loop(0, 2, ring_body, 0)
    for m in range(2):
        for d in range(2):
            hop_in(d, half, m).wait_recv()
            share(d, half, m, core).start()

        def last_body(j, _, m=m):
            b = at(pos + half, lax.rem(core + j, 2))

            @pl.when(j == 1)
            def _():
                for d in range(2):
                    share(d, half, m, 1 - core).wait_recv()
            part = compute(b, *ends[0][m]) + compute(b, *ends[1][m])
            send_buf[b] = part if m == 0 else send_buf[b] + part
            if m == 1:
                score_copy(b).start()
            return 0

        lax.fori_loop(0, 2, last_body, 0)

    for k in range(2):
        share(0, 0, k, core).wait_send()
        for d in range(2):
            for s in range(1, half + 1):
                hop(d, s, k).wait_send()
                share(d, s, k, core).wait_send()
    each(1, lambda o: id_copy(o).wait_send())
    each(1, lambda o: score_copy(lax.rem(me + o, n)).wait_send())
    each(1, lambda o: score_in(o).wait_recv())
    out_ref[...] = got[...].reshape(out_ref.shape)
    place_ref[...] = place[...]


def finish(got_ref, place_ref, out_ref, best_ref):
    spread = None
    for part in split3(got_ref[...]):
        term = jnp.dot(place_ref[...], part, preferred_element_type=jnp.float32)
        spread = term if spread is None else spread + term
    queries = out_ref.shape[0]
    out_ref[...] = spread.T[:queries]
    best_ref[...] = sort_down(spread).T[:queries, :best_ref.shape[1]]


def local(ways, queries, passages, lengths, candidates):
    n = lax.axis_size("corpus")
    per_owner, tile_rows, feature = passages.shape
    per_device, tok = queries.shape[0], queries.shape[1]
    number = candidates.shape[1]
    rows = per_device * tok
    cap = max(2, 3 * number // (2 * n))
    slots = -(-cap // 8) * 8
    col = pick_tile(rows, tok)
    half = n // 4
    cfg = (n, ways, cap, per_owner, tile_rows, rows, feature, tok, col)
    got, place = pl.pallas_call(
        functools.partial(kernel, cfg),
        out_shape=(
            jax.ShapeDtypeStruct((n * slots, 128), jnp.float32),
            jax.ShapeDtypeStruct((number, n * slots), jnp.bfloat16),
        ),
        in_specs=[
            pl.BlockSpec(memory_space=pltpu.VMEM),
            pl.BlockSpec(memory_space=pltpu.SMEM),
            pl.BlockSpec(memory_space=pl.ANY),
            pl.BlockSpec(memory_space=pl.ANY),
        ],
        out_specs=(
            pl.BlockSpec(memory_space=pltpu.VMEM),
            pl.BlockSpec(memory_space=pltpu.VMEM),
        ),
        scratch_shapes=[
            pltpu.VMEM((n, rows, feature), queries.dtype),
            pltpu.VMEM(passages.shape, passages.dtype),
            pltpu.VMEM((n, 1, number), jnp.int32),
            pltpu.VMEM((n, number), jnp.int32),
            pltpu.SMEM((n, number), jnp.int32),
            pltpu.VMEM((number, n * slots), jnp.bfloat16),
            pltpu.VMEM((rows, 128), jnp.bfloat16),
            pltpu.VMEM((n, slots, 128), jnp.float32),
            pltpu.VMEM((n, slots, 128), jnp.float32),
            pltpu.SemaphoreType.DMA((2, half + 1, 2)),
            pltpu.SemaphoreType.DMA((2, half + 1, 2)),
            pltpu.SemaphoreType.DMA((2, half + 1, 2)),
            pltpu.SemaphoreType.DMA((2, half + 1, 2)),
            pltpu.SemaphoreType.DMA((n,)),
            pltpu.SemaphoreType.DMA((n,)),
            pltpu.SemaphoreType.DMA((n,)),
            pltpu.SemaphoreType.DMA((n,)),
            pltpu.SemaphoreType.DMA((4,)),
        ],
        compiler_params=pltpu.CompilerParams(
            collective_id=0, has_side_effects=True, vmem_limit_bytes=60 * 2**20),
    )(candidates, lengths, queries.reshape(rows, feature), passages)
    return pl.pallas_call(
        finish,
        out_shape=(
            jax.ShapeDtypeStruct((per_device, number), jnp.float32),
            jax.ShapeDtypeStruct((per_device, TOPK), jnp.float32),
        ),
        in_specs=[pl.BlockSpec(memory_space=pltpu.VMEM)] * 2,
        out_specs=(pl.BlockSpec(memory_space=pltpu.VMEM), pl.BlockSpec(memory_space=pltpu.VMEM)),
    )(got, place)


def solution(mesh):
    ways = 2 if mesh.shape["groups"] == 2 else 1
    return jax.shard_map(
        functools.partial(local, ways),
        mesh=mesh,
        in_specs=(
            P(("groups", "corpus"), None, None),
            P(("groups", "corpus"), None, None),
            P(("groups", "corpus")),
            P(("groups", "corpus"), None),
        ),
        out_specs=(P(("groups", "corpus"), None), P(("groups", "corpus"), None)),
        check_vma=False,
    )
```

```python
import functools

import jax
import jax.numpy as jnp
from jax import lax
from jax.experimental import pallas as pl
from jax.experimental.pallas import tpu as pltpu
from jax.sharding import PartitionSpec as P

TOPK = 100
MESH = pl.DeviceIdType.MESH


def pick_tile(rows, tok):
    tile = 256
    while rows % tile or tile % tok:
        tile //= 2
    return tile


def sort_down(x):
    count, width = x.shape
    index = lax.broadcasted_iota(jnp.int32, (count // 8, 8, width), 0) * 8
    index = index + lax.broadcasted_iota(jnp.int32, (count // 8, 8, width), 1)
    x = x.reshape(count // 8, 8, width)
    size = 2
    while size <= count:
        gap = size // 2
        falling = (index // size) % 2 == 0
        while gap >= 1:
            low = (index // gap) % 2 == 0
            if gap >= 8:
                hop = gap // 8
                y = x.reshape(count // (2 * gap), 2, hop, 8, width)
                y = jnp.concatenate([y[:, 1:], y[:, :1]], axis=1)
                other = y.reshape(x.shape)
            else:
                other = jnp.where(low, pltpu.roll(x, 8 - gap, 1), pltpu.roll(x, gap, 1))
            x = jnp.where(low == falling, jnp.maximum(x, other), jnp.minimum(x, other))
            gap //= 2
        size *= 2
    return x.reshape(count, width)


def split3(x):
    high = x.astype(jnp.bfloat16)
    rest = x - high.astype(jnp.float32)
    mid = rest.astype(jnp.bfloat16)
    low = (rest - mid.astype(jnp.float32)).astype(jnp.bfloat16)
    return high, mid, low


def kernel(cfg, cand_ref, len_ref, q_hbm, p_hbm, out_ref, place_ref, qall, pas, cand_all,
           wanted_v, wanted_s, place, fold, send_buf, got, q_send, q_recv,
           sib_send, sib_recv, id_send, id_recv, sc_send, sc_recv, loc_sem):
    n, ways, cap, per_owner, tile_rows, rows, feature, tok, col = cfg
    chips = n // 2
    half = chips // 2
    depth = chips // ways
    units = rows // col
    cut = (units + 1) // 2
    spans = ((0, cut), (cut, units))
    ends = tuple(((lo, (lo + hi + 1) // 2), ((lo + hi + 1) // 2, hi)) for lo, hi in spans)
    me = lax.axis_index("corpus")
    core = lax.rem(me, 2)
    chip = me // 2
    if ways == 2:
        zz, yy = chip // 2, lax.rem(chip, 2)
        pos = (1 - yy) * zz + yy * (2 * depth - 1 - zz)
    else:
        pos = chip

    def at(p, c):
        p = lax.rem(p + 2 * chips, chips)
        if ways == 2:
            far = p // depth
            p = (1 - far) * (2 * p) + far * ((2 * depth - 1 - p) * 2 + 1)
        return p * 2 + c

    sib = at(pos, 1 - core)
    right, left = at(pos + 1, core), at(pos - 1, core)
    toward = (right, left)

    def origin(d, s, c):
        return at(pos - s if d == 0 else pos + s, c)

    def piece(b, d, s, k):
        lo, hi = ends[d][k] if s == half else spans[k]
        return qall.at[b, pl.ds(lo * col, (hi - lo) * col), :]

    def hop(d, s, k):
        b = origin(d, s - 1, core)
        return pltpu.make_async_remote_copy(
            src_ref=piece(b, d, s, k), dst_ref=piece(b, d, s, k),
            send_sem=q_send.at[d, s, k], recv_sem=q_recv.at[d, s, k],
            device_id={"corpus": toward[d]}, device_id_type=MESH)

    def hop_in(d, s, k):
        b = origin(d, s, core)
        return pltpu.make_async_remote_copy(
            src_ref=piece(b, d, s, k), dst_ref=piece(b, d, s, k),
            send_sem=q_send.at[d, s, k], recv_sem=q_recv.at[d, s, k],
            device_id={"corpus": toward[d]}, device_id_type=MESH)

    def share(d, s, k, c):
        b = origin(d, s, c)
        return pltpu.make_async_remote_copy(
            src_ref=piece(b, d, s, k), dst_ref=piece(b, d, s, k),
            send_sem=sib_send.at[d, s, k], recv_sem=sib_recv.at[d, s, k],
            device_id={"corpus": sib}, device_id_type=MESH)

    def id_copy(o):
        peer = lax.rem(me + o, n)
        return pltpu.make_async_remote_copy(
            src_ref=cand_all.at[me], dst_ref=cand_all.at[me],
            send_sem=id_send.at[o], recv_sem=id_recv.at[me],
            device_id={"corpus": peer}, device_id_type=MESH)

    def id_in(o):
        peer = lax.rem(me + o, n)
        return pltpu.make_async_remote_copy(
            src_ref=cand_all.at[peer], dst_ref=cand_all.at[peer],
            send_sem=id_send.at[o], recv_sem=id_recv.at[peer],
            device_id={"corpus": peer}, device_id_type=MESH)

    def score_copy(b):
        return pltpu.make_async_remote_copy(
            src_ref=send_buf.at[b], dst_ref=got.at[me],
            send_sem=sc_send.at[b], recv_sem=sc_recv.at[me],
            device_id={"corpus": b}, device_id_type=MESH)

    def score_in(o):
        peer = lax.rem(me + o, n)
        return pltpu.make_async_remote_copy(
            src_ref=send_buf.at[peer], dst_ref=got.at[peer],
            send_sem=sc_send.at[peer], recv_sem=sc_recv.at[peer],
            device_id={"corpus": peer}, device_id_type=MESH)

    q_load = pltpu.make_async_copy(q_hbm, qall.at[me], loc_sem.at[0])
    c_load = pltpu.make_async_copy(cand_ref, cand_all.at[me], loc_sem.at[2])
    p_load = pltpu.make_async_copy(p_hbm, pas, loc_sem.at[1])
    c_load.start()
    q_load.start()
    p_load.start()

    barrier = pltpu.get_barrier_semaphore()

    def greet(o, _):
        pl.semaphore_signal(barrier, inc=1, device_id={"corpus": lax.rem(me + o, n)},
                            device_id_type=MESH)
        return 0

    lax.fori_loop(1, n, greet, 0)
    c_load.wait()
    q_load.wait()
    pl.semaphore_wait(barrier, n - 1)

    def each(first, fn):
        def body(o, _):
            fn(o)
            return 0
        lax.fori_loop(first, n, body, 0)

    each(1, lambda o: id_copy(o).start())
    for k in range(2):
        for d in range(2):
            hop(d, 1, k).start()
        share(0, 0, k, core).start()
    row_at = lax.broadcasted_iota(jnp.int32, (rows, 128), 0) // tok
    lane_at = lax.broadcasted_iota(jnp.int32, (rows, 128), 1)
    fold[...] = jnp.where(row_at == lane_at, 1.0, 0.0).astype(fold.dtype)
    slots = send_buf.shape[1]
    number = cand_ref.shape[1]
    mine_row = lax.div(cand_ref[...], per_owner).astype(jnp.float32)
    across = jnp.broadcast_to(mine_row, (number, number))
    down = across.T
    r_at = lax.broadcasted_iota(jnp.int32, (number, number), 0)
    c_at = lax.broadcasted_iota(jnp.int32, (number, number), 1)
    ahead = jnp.where((across == down) & (c_at < r_at), 1.0, 0.0)
    slot = down[:, :1] * float(slots) + jnp.sum(ahead, axis=1, keepdims=True)
    slot_at = lax.broadcasted_iota(jnp.int32, place.shape, 1).astype(jnp.float32)
    place[...] = jnp.where(slot_at == slot, 1.0, 0.0).astype(place.dtype)
    in_tile = lax.broadcasted_iota(jnp.int32, (tile_rows, feature), 0)
    p_load.wait()

    def fill(i, _):
        for j in range(4):
            p = i * 4 + j
            tile = pas[p].astype(jnp.float32)
            tile = jnp.where(in_tile < len_ref[p], tile, tile[0:1, :])
            pas[p] = tile.astype(pas.dtype)
        return 0

    lax.fori_loop(0, per_owner // 4, fill, 0)
    each(1, lambda o: id_in(o).wait_recv())

    ids = cand_all[...].reshape(n, cand_all.shape[2])
    owner = lax.div(ids, per_owner)
    local = ids - owner * per_owner
    mine = owner == me
    before = jnp.where(r_at < c_at, 1.0, 0.0).astype(jnp.bfloat16)
    rank = jnp.dot(jnp.where(mine, 1.0, 0.0).astype(jnp.bfloat16), before,
                   preferred_element_type=jnp.float32)
    lane = lax.broadcasted_iota(jnp.int32, (n, number), 1)
    wanted = jnp.zeros((n, number), jnp.int32)
    for s in range(cap):
        hit = mine & (rank == float(s))
        found = jnp.max(jnp.where(hit, local, 0), axis=1, keepdims=True)
        wanted = jnp.where(lane == s, found, wanted)
    wanted_v[...] = wanted
    w_load = pltpu.make_async_copy(wanted_v, wanted_s, loc_sem.at[3])
    w_load.start()
    w_load.wait()

    def compute(b, lo, hi):
        chosen = [wanted_s[b, s] for s in range(cap)]
        pieces = []
        for u in range(lo, hi):
            qs = qall[b, pl.ds(u * col, col), :]
            near = []
            for s in range(cap):
                sim = lax.dot_general(pas[chosen[s]], qs, (((1,), (1,)), ((), ())),
                                      preferred_element_type=jnp.float32)
                near.append(jnp.max(sim, axis=0, keepdims=True))
            if cap < slots:
                near.append(jnp.zeros((slots - cap, col), jnp.float32))
            near = jnp.concatenate(near, axis=0)
            high = near.astype(jnp.bfloat16).astype(jnp.float32)
            pieces.append(jnp.concatenate([high, near - high], axis=0).astype(jnp.bfloat16))
        part = jnp.dot(jnp.concatenate(pieces, axis=1), fold[pl.ds(lo * col, (hi - lo) * col), :],
                       preferred_element_type=jnp.float32)
        return (part[:slots] + part[slots:]) / float(tok)

    for k in range(2):
        share(0, 0, k, 1 - core).wait_recv()

    def near_body(j, _):
        b = at(pos, lax.rem(core + j, 2))
        send_buf[b] = compute(b, *spans[0]) + compute(b, *spans[1])

        @pl.when(j == 1)
        def _():
            score_copy(b).start()
        return 0

    lax.fori_loop(0, 2, near_body, 0)
    got[me] = send_buf[me]

    for s in range(1, half):
        for k in range(2):
            for d in range(2):
                hop_in(d, s, k).wait_recv()
                if s + 1 < half:
                    hop(d, s + 1, k).start()
                elif k == d:
                    for m in range(2):
                        hop(d, half, m).start()
                share(d, s, k, core).start()

            def ring_body(j, _, s=s, k=k):
                @pl.when(j == 1)
                def _():
                    for d in range(2):
                        share(d, s, k, 1 - core).wait_recv()
                blocks = [origin(d, s, lax.rem(core + j, 2)) for d in range(2)]
                found = [compute(b, *spans[k]) for b in blocks]
                for b, part in zip(blocks, found):
                    send_buf[b] = part if k == 0 else send_buf[b] + part
                if k == 1:
                    for b in blocks:
                        score_copy(b).start()
                return 0

            lax.fori_loop(0, 2, ring_body, 0)
    for m in range(2):
        for d in range(2):
            hop_in(d, half, m).wait_recv()
            share(d, half, m, core).start()

        def last_body(j, _, m=m):
            b = at(pos + half, lax.rem(core + j, 2))

            @pl.when(j == 1)
            def _():
                for d in range(2):
                    share(d, half, m, 1 - core).wait_recv()
            part = compute(b, *ends[0][m]) + compute(b, *ends[1][m])
            send_buf[b] = part if m == 0 else send_buf[b] + part
            if m == 1:
                score_copy(b).start()
            return 0

        lax.fori_loop(0, 2, last_body, 0)

    for k in range(2):
        share(0, 0, k, core).wait_send()
        for d in range(2):
            for s in range(1, half + 1):
                hop(d, s, k).wait_send()
                share(d, s, k, core).wait_send()
    each(1, lambda o: id_copy(o).wait_send())
    each(1, lambda o: score_copy(lax.rem(me + o, n)).wait_send())
    each(1, lambda o: score_in(o).wait_recv())
    out_ref[...] = got[...].reshape(out_ref.shape)
    place_ref[...] = place[...]


def finish(got_ref, place_ref, out_ref, best_ref):
    spread = None
    for part in split3(got_ref[...]):
        term = jnp.dot(place_ref[...], part, preferred_element_type=jnp.float32)
        spread = term if spread is None else spread + term
    queries = out_ref.shape[0]
    out_ref[...] = spread.T[:queries]
    best_ref[...] = sort_down(spread).T[:queries, :best_ref.shape[1]]


def local(ways, queries, passages, lengths, candidates):
    n = lax.axis_size("corpus")
    per_owner, tile_rows, feature = passages.shape
    per_device, tok = queries.shape[0], queries.shape[1]
    number = candidates.shape[1]
    rows = per_device * tok
    cap = max(2, 3 * number // (2 * n))
    slots = -(-cap // 8) * 8
    col = pick_tile(rows, tok)
    half = n // 4
    cfg = (n, ways, cap, per_owner, tile_rows, rows, feature, tok, col)
    got, place = pl.pallas_call(
        functools.partial(kernel, cfg),
        out_shape=(
            jax.ShapeDtypeStruct((n * slots, 128), jnp.float32),
            jax.ShapeDtypeStruct((number, n * slots), jnp.bfloat16),
        ),
        in_specs=[
            pl.BlockSpec(memory_space=pltpu.VMEM),
            pl.BlockSpec(memory_space=pltpu.SMEM),
            pl.BlockSpec(memory_space=pl.ANY),
            pl.BlockSpec(memory_space=pl.ANY),
        ],
        out_specs=(
            pl.BlockSpec(memory_space=pltpu.VMEM),
            pl.BlockSpec(memory_space=pltpu.VMEM),
        ),
        scratch_shapes=[
            pltpu.VMEM((n, rows, feature), queries.dtype),
            pltpu.VMEM(passages.shape, passages.dtype),
            pltpu.VMEM((n, 1, number), jnp.int32),
            pltpu.VMEM((n, number), jnp.int32),
            pltpu.SMEM((n, number), jnp.int32),
            pltpu.VMEM((number, n * slots), jnp.bfloat16),
            pltpu.VMEM((rows, 128), jnp.bfloat16),
            pltpu.VMEM((n, slots, 128), jnp.float32),
            pltpu.VMEM((n, slots, 128), jnp.float32),
            pltpu.SemaphoreType.DMA((2, half + 1, 2)),
            pltpu.SemaphoreType.DMA((2, half + 1, 2)),
            pltpu.SemaphoreType.DMA((2, half + 1, 2)),
            pltpu.SemaphoreType.DMA((2, half + 1, 2)),
            pltpu.SemaphoreType.DMA((n,)),
            pltpu.SemaphoreType.DMA((n,)),
            pltpu.SemaphoreType.DMA((n,)),
            pltpu.SemaphoreType.DMA((n,)),
            pltpu.SemaphoreType.DMA((4,)),
        ],
        compiler_params=pltpu.CompilerParams(
            collective_id=0, has_side_effects=True, vmem_limit_bytes=60 * 2**20),
    )(candidates, lengths, queries.reshape(rows, feature), passages)
    return pl.pallas_call(
        finish,
        out_shape=(
            jax.ShapeDtypeStruct((per_device, number), jnp.float32),
            jax.ShapeDtypeStruct((per_device, TOPK), jnp.float32),
        ),
        in_specs=[pl.BlockSpec(memory_space=pltpu.VMEM)] * 2,
        out_specs=(pl.BlockSpec(memory_space=pltpu.VMEM), pl.BlockSpec(memory_space=pltpu.VMEM)),
    )(got, place)


def solution(mesh):
    ways = 2 if mesh.shape["groups"] == 2 else 1
    return jax.shard_map(
        functools.partial(local, ways),
        mesh=mesh,
        in_specs=(
            P(("groups", "corpus"), None, None),
            P(("groups", "corpus"), None, None),
            P(("groups", "corpus")),
            P(("groups", "corpus"), None),
        ),
        out_specs=(P(("groups", "corpus"), None), P(("groups", "corpus"), None)),
        check_vma=False,
    )
```
